128 devices in a mesh: ctx: 8 (over x, z_lo), exp: 16 (over y, z_hi, core).
Axes of the slice: x: 4, y: 4, z: 4 (z_hi: 2, z_lo: 2; z = z_hi * 2 + z_lo), core: 2. Of those that a mesh axis runs over, the one named last changes fastest.
Arguments:
- queries: bfloat16 [16, 1024, 2048], P('exp', 'ctx')
- key_rows: bfloat16 [16, 1024, 2048], P('exp', 'ctx')
- value_rows: bfloat16 [16, 1024, 2048], P('exp', 'ctx'), may hold values from -6 to 6
- out_grad: bfloat16 [16, 1024, 2048], P('exp', 'ctx'), may hold values from -6 to 6
- moe_input: bfloat16 [16, 1024, 2048], P('exp', 'ctx'), may hold values from -6 to 6
- routes: int32 [16, 1024, 4], P('exp', 'ctx'), may hold values from 0 to 31, all different within a row; in each aligned block of 128 rows (0 to 127, 128 to 255, ..., all dimensions but the last counted through in order) at most 24 rows name the same one
- route_gates: float32 [16, 1024, 4], P('exp', 'ctx'), may hold values from 0.1 to 1
- up_weight: bfloat16 [32, 2048, 768], P('exp'), may hold values from -0.125 to 0.125
- down_weight: bfloat16 [32, 768, 2048], P('exp'), may hold values from -0.21875 to 0.21875
Outputs:
- query_grad: bfloat16 [16, 1024, 2048], P('exp', 'ctx')
- key_grad: bfloat16 [16, 1024, 2048], P('exp', 'ctx')
- value_grad: bfloat16 [16, 1024, 2048], P('exp', 'ctx')
- input_grad: bfloat16 [16, 1024, 2048], P('exp', 'ctx')
The draws below stay inside these ranges and needn't reach their ends.
Inputs may be any that keep to these rules, and one draw needn't show every extreme that they name: In the bins of one device no expert is named by more than 24 routes, a bound that some block reaches; the 4 experts of a bin differ.
All inputs are finite; a program needn't handle non-finite values.
Results may differ from the reference program's by a relative error of at most 0.0064.
Values may be sent and summed in bfloat16 or wider, within the bound.
A program may use at most 128 MiB of HBM per device.

```python
import math
import jax
import jax.numpy as jnp
import numpy as np
from jax import lax

H = 16
HD = 128
D = 2048
EXPERTS = 32
FFH = 768
TOPK = 4
BINS_DEV = 128
CAP = 24
L = 1024
SEQS = 16
N_CTX = 8


def drawn_pair(key):
    head_shape = (SEQS, L, H, HD)
    query_draw = jax.random.truncated_normal(jax.random.fold_in(key, 1), -5.0, 5.0, head_shape, jnp.float32) * 1.4
    key_draw = jax.random.truncated_normal(jax.random.fold_in(key, 2), -5.0, 5.0, head_shape, jnp.float32) * 1.4
    return (query_draw.reshape(SEQS, L, D), key_draw.reshape(SEQS, L, D))


def draw_queries(key, part):
    return drawn_pair(key)[0].astype(jnp.bfloat16)


def draw_key_rows(key, part):
    return drawn_pair(key)[1].astype(jnp.bfloat16)


def block_scale(own_key, shape, split, low, high):
    loudness = 1.0
    for position, shards_of in split:
        heights = jax.random.uniform(jax.random.fold_in(jax.random.fold_in(own_key, 6), position), (shards_of,), jnp.float32, low / len(split), high / len(split))
        loudness = loudness * jnp.repeat(jnp.exp(heights), shape[position] // shards_of).reshape((-1,) + (1,) * (len(shape) - 1 - position))
    return loudness


def routed_block(stream_key, own, number, rows, count, top, limit, skew):
    ranking = jax.random.permutation(stream_key, count)
    packed, ordinary = load_shares(count, rows * top, limit, skew, True), load_shares(count, rows * top, limit, skew, False)
    places = jnp.arange(count)

    def named(sizes, offset_by):
        used = int((sizes > 0).sum())
        fixed = max(1, used // 4)
        shifted = fixed + (places - fixed + offset_by * (used - fixed)) % max(1, count - fixed)
        return jnp.zeros((count,), jnp.int32).at[ranking[jnp.where(places < fixed, places, shifted)]].set(jnp.asarray(sizes, jnp.int32))

    sizes = jnp.where(number % 4 == 0, named(packed, number // 4), named(ordinary, number - number // 4 - 1))
    mixed = jax.random.permutation(jax.random.fold_in(own, 3), count)
    donor, sink = mixed[0:count // 2 * 2:2], mixed[1:count // 2 * 2:2]
    margin = jnp.minimum(sizes[donor] - 1, limit - sizes[sink]) // 2
    margin = jnp.where((donor == ranking[0]) | (sink == ranking[0]) | (sizes[sink] == 0), 0, jnp.maximum(margin, 0))
    shifted = jax.random.randint(jax.random.fold_in(own, 4), (count // 2,), 0, 1 << 20) % (margin + 1)
    sizes = sizes.at[donor].add(-shifted).at[sink].add(shifted)
    members = jnp.searchsorted(jnp.cumsum(sizes), jnp.arange(rows * top), side="right").astype(jnp.int32)
    listing = members.reshape(top, rows).T
    listing = listing[jax.random.permutation(jax.random.fold_in(own, 1), rows)]
    offset_by = jax.random.randint(jax.random.fold_in(own, 2), (rows, 1), 0, top)
    return jnp.take_along_axis(listing, (jnp.arange(top)[None, :] + offset_by) % top, axis=1)


def load_shares(count, total, limit, slope, full):
    weights = [(1 << 20) // math.isqrt(grade ** slope) + 1 for grade in range(1, count + 1)]
    largest = limit if full else min(limit, max(-(-total // count), total * weights[0] // sum(weights)))
    least = 1 if total - largest >= count - 1 else 0
    given, surplus = [largest] + [least] * (count - 1), total - largest - least * (count - 1)
    while surplus > 0:
        candidates = [i for i in range(1, count) if given[i] < largest] or [i for i in range(1, count) if given[i] < limit]
        pool, left = sum([weights[i] for i in candidates]), surplus
        for i in candidates:
            addition = min(limit - given[i], max(1, left * weights[i] // pool), surplus)
            given[i] = given[i] + addition
            surplus = surplus - addition
    return np.array(given)


def noise(own_key, dims, deviation, limit, split=(), kind=jnp.bfloat16):
    array = jax.random.normal(own_key, dims, jnp.float32) * deviation
    if len(split) > 0:
        array = block_scale(own_key, dims, split, -0.22, 0.18) * array
    return jnp.clip(array, min=-limit, max=limit).astype(kind)


def setup_inputs(seed: int = 0) -> dict:
    seeds = jax.random.split(jax.random.key(seed), 10)
    queries = draw_queries(jax.random.fold_in(seeds[9], 71), 0)
    key_rows = draw_key_rows(jax.random.fold_in(seeds[9], 71), 0)
    value_rows = noise(seeds[2], (SEQS, L, D), 1.0, 6.0, ((0, 16), (1, 8)))
    out_grad = jnp.clip(jax.random.uniform(seeds[3], (SEQS, L, D), jnp.float32, -6.0, 6.0) * block_scale(seeds[3], (SEQS, L, D), ((0, 16), (1, 8)), -0.4, 0.0), -6.0, 6.0).astype(jnp.bfloat16)
    moe_input = noise(seeds[4], (SEQS, L, D), 1.0, 6.0, ((0, 16), (1, 8)))
    routes_keys = jax.random.split(jax.random.fold_in(seeds[5], 1), SEQS * L // BINS_DEV)
    routes_turns = jax.random.permutation(jax.random.fold_in(seeds[5], 3), SEQS * L // BINS_DEV)
    routes = jax.vmap(lambda own, number: routed_block(jax.random.fold_in(seeds[5], 2), own, number, BINS_DEV, EXPERTS, TOPK, CAP, 2))(routes_keys, routes_turns).reshape((SEQS, L, TOPK))
    route_gates = jnp.clip(jnp.exp(math.log(1.0) - 2.3025851 * jax.random.uniform(seeds[6], (SEQS, L, TOPK), jnp.float32) ** block_scale(seeds[6], (SEQS, L, TOPK), ((0, 16), (1, 8)), -0.2, 0.2)), 0.1, 1.0)
    up_weight = noise(seeds[7], (EXPERTS, D, FFH), D ** -0.5, 0.125, ((0, 16),))
    down_weight = noise(seeds[8], (EXPERTS, FFH, D), FFH ** -0.5, 0.21875, ((0, 16),))
    return dict(queries=queries, key_rows=key_rows, value_rows=value_rows, out_grad=out_grad, moe_input=moe_input, routes=routes, route_gates=route_gates, up_weight=up_weight, down_weight=down_weight)


def head_back(operands):
    query_head, key_head, value_head, grad_head = operands
    score_scale = HD ** -0.5
    scores = jnp.dot(query_head, key_head.T, preferred_element_type=jnp.float32) * score_scale
    probs = jax.nn.softmax(scores, axis=-1)
    rounded = probs.astype(jnp.bfloat16)
    prob_grad = jnp.dot(grad_head, value_head.T, preferred_element_type=jnp.float32)
    row_delta = jnp.sum(probs * prob_grad, axis=-1, keepdims=True)
    score_grad = (probs * (prob_grad - row_delta)).astype(jnp.bfloat16)
    query_part = (jnp.dot(score_grad, key_head, preferred_element_type=jnp.float32) * score_scale).astype(jnp.bfloat16)
    key_part = (jnp.dot(score_grad.T, query_head, preferred_element_type=jnp.float32) * score_scale).astype(jnp.bfloat16)
    value_part = jnp.dot(rounded.T, grad_head, preferred_element_type=jnp.float32).astype(jnp.bfloat16)
    return query_part, key_part, value_part


def to_heads(member):
    return member.reshape(SEQS, L, H, HD).transpose(0, 2, 1, 3).reshape(SEQS * H, L, HD)


def from_heads(member):
    return member.reshape(SEQS, H, L, HD).transpose(0, 2, 1, 3).reshape(SEQS, L, D)


def reference(queries, key_rows, value_rows, out_grad, moe_input, routes, route_gates, up_weight, down_weight):
    query_parts, key_parts, value_parts = lax.map(head_back, (to_heads(queries), to_heads(key_rows), to_heads(value_rows), to_heads(out_grad)))
    flat_routes = routes.reshape(-1).astype(jnp.int32)
    route_total = flat_routes.shape[0]
    expert_most = SEQS * N_CTX * CAP
    zero_row = jnp.zeros((1, D), jnp.bfloat16)
    padded_inputs = jnp.concatenate([moe_input.reshape(SEQS * L, D), zero_row], axis=0)
    padded_grads = jnp.concatenate([out_grad.reshape(SEQS * L, D), zero_row], axis=0)
    padded_gates = jnp.concatenate([route_gates.reshape(-1), jnp.zeros((1,), jnp.float32)])

    def one_expert(carried, expert):
        chosen = jnp.nonzero(flat_routes == expert, size=expert_most, fill_value=route_total)[0].astype(jnp.int32)
        token_index = (chosen // TOPK).astype(jnp.int32)
        rows_in = padded_inputs[token_index]
        gate_values = padded_gates[chosen]
        gated_rows = (gate_values[:, None] * padded_grads[token_index].astype(jnp.float32)).astype(jnp.bfloat16)
        up_matrix = up_weight[expert]
        down_matrix = down_weight[expert]
        preact = jnp.dot(rows_in, up_matrix, preferred_element_type=jnp.float32)
        sigmoid = jax.nn.sigmoid(preact)
        slopes = sigmoid * (1.0 + preact * (1.0 - sigmoid))
        back_grad = jnp.dot(gated_rows, down_matrix.T, preferred_element_type=jnp.float32)
        hidden_grad = (back_grad * slopes).astype(jnp.bfloat16)
        route_grad = jnp.dot(hidden_grad, up_matrix.T, preferred_element_type=jnp.float32).astype(jnp.bfloat16)
        carried = carried.at[token_index].add(route_grad.astype(jnp.float32))
        return carried, None

    initial = jnp.zeros((SEQS * L + 1, D), jnp.float32)
    summed, unused = lax.scan(one_expert, initial, jnp.arange(EXPERTS, dtype=jnp.int32))
    input_grad = summed[:-1].reshape(SEQS, L, D).astype(jnp.bfloat16)
    return (from_heads(query_parts), from_heads(key_parts), from_heads(value_parts), input_grad)
```

```python
import functools

import jax
import jax.numpy as jnp
from jax import lax
from jax.experimental import pallas as pl
from jax.experimental.pallas import tpu as pltpu
from jax.sharding import PartitionSpec as P

HD = 128
CAP = 24
MESH = pl.DeviceIdType.MESH
F32 = jnp.float32
BF16 = jnp.bfloat16
N_COPIES = 96


def dot_nn(a, b):
    return lax.dot_general(a, b, (((1,), (0,)), ((), ())), preferred_element_type=F32)


def dot_nt(a, b):
    return lax.dot_general(a, b, (((1,), (1,)), ((), ())), preferred_element_type=F32)


def dot_tn(a, b):
    return lax.dot_general(a, b, (((0,), (0,)), ((), ())), preferred_element_type=F32)


def kernel(
    q_ref, k_ref, v_ref, g_ref, x_ref, meta_ref, up_ref, down_ref,
    dq_ref, dk_ref, dv_ref, dx_ref,
    aq, ak, av, ag, oq, ok, ov, dk_acc, dv_acc,
    xb, gb, mb, w_up, w_down, xs, gs, sel, gcol, hid, rg, part,
    ra1, ra2, ra3, rb1, rb2, rb3,
    send_sem, recv_sem, local_sem,
):
    ctx = lax.axis_index("ctx")
    exp = lax.axis_index("exp")
    n_ctx = 8
    bins, width = x_ref.shape
    head_cols = width // n_ctx
    half_rows = bins // 2
    half_cols = width // 2
    z_lo = lax.rem(ctx, 2)
    row_x = ctx - z_lo
    core = lax.rem(exp, 2)
    z_hi = lax.rem(exp // 2, 2)
    y = exp // 4
    rest = exp - y * 4

    def at_y(offset):
        return {"ctx": ctx, "exp": lax.rem(y + offset, 4) * 4 + rest}

    def place(line, offset):
        if line == 0:
            return at_y(offset)
        return {
            "ctx": row_x + 1 - z_lo,
            "exp": lax.rem(y + offset, 4) * 4 + (1 - z_hi) * 2 + core,
        }

    sibling = {"ctx": ctx, "exp": exp + 1 - 2 * core}
    y_next, y_prev, z_other = at_y(1), at_y(3), place(1, 0)

    def ctx_peer(step):
        return {"ctx": lax.rem(ctx + step, n_ctx), "exp": exp}

    barrier = pltpu.get_barrier_semaphore()
    peers = [sibling] + [ctx_peer(s) for s in range(1, n_ctx)]
    peers += [place(line, o) for line in range(2) for o in range(4) if (line, o) != (0, 0)]
    for peer in peers:
        pl.semaphore_signal(barrier, inc=1, device_id=peer, device_id_type=MESH)
    pl.semaphore_wait(barrier, len(peers))

    sent = []

    def send(src, dst, device):
        number = len(sent)
        copy = pltpu.make_async_remote_copy(
            src_ref=src,
            dst_ref=dst,
            send_sem=send_sem.at[number],
            recv_sem=recv_sem.at[number],
            device_id=device,
            device_id_type=MESH,
        )
        copy.start()
        sent.append(copy)
        return copy

    local = []

    def move(src, dst):
        copy = pltpu.make_async_copy(src, dst, local_sem.at[len(local)])
        copy.start()
        local.append(copy)
        return copy

    lo, hi = pl.ds(0, half_rows), pl.ds(half_rows, half_rows)

    def block(ref, line, offset):
        return ref.at[offset, pl.ds(line * bins, bins)]

    def half_block(ref, line, offset, half):
        return ref.at[offset, pl.ds(line * bins + half * half_rows, half_rows)]

    x_z = send(x_ref, block(xb, 1, 0), z_other)
    g_next = send(g_ref, block(gb, 0, 3), y_next)
    g_prev = send(g_ref, block(gb, 0, 1), y_prev)
    metas = []
    for line in range(2):
        for o in range(4):
            if (line, o) != (0, 0):
                metas.append(send(meta_ref, mb.at[(4 - o) % 4, line], place(line, o)))
    own_meta = move(meta_ref, mb.at[0, 0])
    x_next = send(x_ref, block(xb, 0, 3), y_next)
    x_prev = send(x_ref, block(xb, 0, 1), y_prev)
    g_z = [send(g_ref, block(gb, 1, 0), z_other)]

    mine = pl.ds(pl.multiple_of(ctx * head_cols, head_cols), head_cols)
    my_rows = pl.ds(pl.multiple_of(ctx * bins, bins), bins)
    heads_in = []
    for step in range(1, n_ctx):
        there = lax.rem(ctx + step, n_ctx)
        cols = pl.ds(pl.multiple_of(there * head_cols, head_cols), head_cols)
        for src, dst in ((q_ref, aq), (k_ref, ak), (v_ref, av), (g_ref, ag)):
            heads_in.append(send(src.at[:, cols], dst.at[my_rows, :], ctx_peer(step)))
    own_in = []
    for src, dst in ((q_ref, aq), (k_ref, ak), (v_ref, av), (g_ref, ag)):
        own_in.append(move(src.at[:, mine], dst.at[my_rows, :]))
    own_in.append(move(x_ref, block(xb, 0, 0)))
    own_in.append(move(g_ref, block(gb, 0, 0)))

    slots = pl.ds(core * 2, 2)
    weights = [send(up_ref, w_up.at[slots], sibling), send(down_ref, w_down.at[slots], sibling)]
    own_weights = [move(up_ref, w_up.at[slots]), move(down_ref, w_down.at[slots])]

    g_next.wait_recv()
    g_far_next = send(half_block(gb, 0, 3, 0), half_block(gb, 0, 2, 0), y_next)
    g_z.append(send(block(gb, 0, 3), block(gb, 1, 3), z_other))
    g_prev.wait_recv()
    g_far_prev = send(half_block(gb, 0, 1, 1), half_block(gb, 0, 2, 1), y_prev)
    g_z.append(send(block(gb, 0, 1), block(gb, 1, 1), z_other))
    x_z.wait_recv()
    xz_next = send(block(xb, 1, 0), block(xb, 1, 3), y_next)
    xz_prev = send(block(xb, 1, 0), block(xb, 1, 1), y_prev)
    x_next.wait_recv()
    far = [send(half_block(xb, 0, 3, 0), half_block(xb, 0, 2, 0), y_next)]
    x_prev.wait_recv()
    far.append(send(half_block(xb, 0, 1, 1), half_block(xb, 0, 2, 1), y_prev))

    for copy in own_in:
        copy.wait()
    for copy in heads_in:
        copy.wait_recv()
    score_scale = HD ** (-0.5)
    seq_len = aq.shape[0]
    rows = 256

    def one_head(h):
        cols = pl.ds(pl.multiple_of(h * HD, HD), HD)
        dk_acc[...] = jnp.zeros_like(dk_acc)
        dv_acc[...] = jnp.zeros_like(dv_acc)

        def one_block(b, carry):
            own = pl.ds(pl.multiple_of(b * rows, rows), rows)
            queries, grads = aq[own, cols], ag[own, cols]
            keys = ak[:, cols]
            scores = dot_nt(keys, queries) * score_scale
            top = jnp.max(scores, axis=0, keepdims=True)
            powers = jnp.exp(scores - top)
            probs = powers * (1.0 / jnp.sum(powers, axis=0, keepdims=True))
            prob_grad = dot_nt(av[:, cols], grads)
            row_delta = jnp.sum(probs * prob_grad, axis=0, keepdims=True)
            score_grad = (probs * (prob_grad - row_delta)).astype(BF16)
            dv_acc[...] += dot_nn(probs.astype(BF16), grads)
            dk_acc[...] += dot_nn(score_grad, queries)
            query_part = dot_tn(keys, score_grad)
            oq[own, cols] = (query_part.T * score_scale).astype(BF16)
            return carry

        lax.fori_loop(0, seq_len // rows, one_block, 0)
        ok[:, cols] = (dk_acc[...] * score_scale).astype(BF16)
        ov[:, cols] = dv_acc[...].astype(BF16)

    one_head(0)
    g_far_next.wait_recv()
    g_z.append(send(half_block(gb, 0, 2, 0), half_block(gb, 1, 2, 0), z_other))
    g_far_prev.wait_recv()
    g_z.append(send(half_block(gb, 0, 2, 1), half_block(gb, 1, 2, 1), z_other))
    one_head(1)
    heads_out = []
    own_out = []
    for step in range(1, n_ctx):
        there = lax.rem(ctx + step, n_ctx)
        their_rows = pl.ds(pl.multiple_of(there * bins, bins), bins)
        for src, dst in ((oq, dq_ref), (ok, dk_ref), (ov, dv_ref)):
            heads_out.append(send(src.at[their_rows, :], dst.at[:, mine], ctx_peer(step)))
    for src, dst in ((oq, dq_ref), (ok, dk_ref), (ov, dv_ref)):
        own_out.append(move(src.at[my_rows, :], dst.at[:, mine]))

    own_meta.wait()
    for copy in metas:
        copy.wait_recv()
    first_expert = (exp - core) * 2
    pair = 2 * bins
    slot_rows = 2 * CAP
    below = lax.broadcasted_iota(jnp.int32, (pair, pair), 0)
    right = lax.broadcasted_iota(jnp.int32, (pair, pair), 1)
    same = (below // bins) == (right // bins)
    earlier = jnp.where(same & (below < right), 1.0, 0.0).astype(BF16)
    second = (lax.broadcasted_iota(jnp.int32, (1, pair), 1) // bins).astype(F32) * CAP
    slot_ids = lax.broadcasted_iota(jnp.int32, (slot_rows, pair), 0).astype(F32)
    for o in range(4):
        info = jnp.concatenate([mb[o, 0], mb[o, 1]], axis=1)
        hits, gate_rows = [], []
        for e in range(4):
            hit = jnp.where(info[0:4] == (first_expert + e).astype(F32), 1.0, 0.0)
            hits.append(jnp.sum(hit, axis=0, keepdims=True))
            gate_rows.append(jnp.sum(hit * info[4:8], axis=0, keepdims=True))
        named = jnp.concatenate(hits + hits, axis=0)
        rank = dot_nn(named.astype(BF16), earlier)
        for e in range(4):
            target = jnp.where(hits[e] > 0.5, rank[e : e + 1] + second, -1.0)
            chosen = jnp.where(slot_ids == target, 1.0, 0.0)
            these = pl.ds(e * slot_rows, slot_rows)
            sel[o, these, :] = chosen.astype(BF16)
            gate = jnp.sum(chosen * gate_rows[e], axis=1, keepdims=True)
            gcol[o, these, :] = jnp.broadcast_to(gate, (slot_rows, 128))

    xz_next.wait_recv()
    far.append(send(half_block(xb, 1, 3, 0), half_block(xb, 1, 2, 0), y_next))
    xz_prev.wait_recv()
    far.append(send(half_block(xb, 1, 1, 1), half_block(xb, 1, 2, 1), y_prev))

    chunk = 512

    def pick_inputs(o):
        def body(i, carry):
            cols = pl.ds(pl.multiple_of(i * chunk, chunk), chunk)
            picked = dot_nn(sel[o], xb[o, :, cols]).astype(BF16)
            for e in range(4):
                xs[e, pl.ds(o * slot_rows, slot_rows), cols] = picked[e * slot_rows : (e + 1) * slot_rows]
            return carry

        lax.fori_loop(0, width // chunk, body, 0)

    def pick_grads(o):
        gate = gcol[o][:, 0:1]

        def body(i, carry):
            cols = pl.ds(pl.multiple_of(i * chunk, chunk), chunk)
            picked = (dot_nn(sel[o], gb[o, :, cols]) * gate).astype(BF16)
            for e in range(4):
                gs[e, pl.ds(o * slot_rows, slot_rows), cols] = picked[e * slot_rows : (e + 1) * slot_rows]
            return carry

        lax.fori_loop(0, width // chunk, body, 0)

    for o in (0, 1, 3):
        pick_inputs(o)
    for copy in g_z[0:3]:
        copy.wait_recv()
    for o in (0, 1, 3):
        pick_grads(o)
    for copy in own_weights:
        copy.wait()
    for copy in weights:
        copy.wait_recv()
    for copy in far:
        copy.wait_recv()
    pick_inputs(2)
    for copy in g_z[3:5]:
        copy.wait_recv()
    pick_grads(2)

    hidden = up_ref.shape[2]
    tile = 256

    def one_expert(e, carry):
        def inner(n, carry):
            cols = pl.ds(pl.multiple_of(n * tile, tile), tile)
            preact = dot_nn(xs[e], w_up[e, :, cols])
            sigmoid = jax.nn.sigmoid(preact)
            slopes = sigmoid * (1.0 + preact * (1.0 - sigmoid))
            back_grad = dot_nt(gs[e], w_down[e, cols, :])
            hid[:, cols] = (back_grad * slopes).astype(BF16)
            return carry

        lax.fori_loop(0, hidden // tile, inner, 0)

        def outer(n, carry):
            cols = pl.ds(pl.multiple_of(n * chunk, chunk), chunk)
            made = dot_nt(hid[...], w_up[e, cols, :]).astype(BF16)
            these = pl.ds(pl.multiple_of(e * slot_rows, slot_rows), slot_rows)
            for o in range(4):
                rg[o, these, cols] = made[o * slot_rows : (o + 1) * slot_rows]
            return carry

        lax.fori_loop(0, width // chunk, outer, 0)
        return carry

    lax.fori_loop(0, 4, one_expert, 0)

    def put_back(o):
        def body(i, carry):
            cols = pl.ds(pl.multiple_of(i * chunk, chunk), chunk)
            part[o, :, cols] = dot_tn(sel[o], rg[o, :, cols]).astype(BF16)
            return carry

        lax.fori_loop(0, width // chunk, body, 0)

    left, right_cols = pl.ds(0, half_cols), pl.ds(half_cols, half_cols)

    def view(line, o, cols, half=None):
        if half is None:
            return part.at[o, pl.ds(line * bins, bins), cols]
        return part.at[o, pl.ds(line * bins + half * half_rows, half_rows), cols]

    def add_into(target, *others):
        total = target[...].astype(F32)
        for other in others:
            total = total + other[...].astype(F32)
        target[...] = total.astype(BF16)

    put_back(2)
    a1, b1 = {}, {}
    for line in range(2):
        a1[line, 0] = send(view(line, 2, left, 0), ra1.at[line, 0], y_next)
        a1[line, 1] = send(view(line, 2, left, 1), ra1.at[line, 1], y_prev)
    b1[2] = send(view(1, 2, right_cols), rb1.at[2], z_other)
    for o in (1, 3):
        put_back(o)
        b1[o] = send(view(1, o, right_cols), rb1.at[o], z_other)
    put_back(0)
    b1[0] = send(view(1, 0, right_cols), rb1.at[0], z_other)

    a2 = {}
    for line in (1, 0):
        a1[line, 0].wait_recv()
        add_into(view(line, 1, left, 0), ra1.at[line, 0])
        a2[line, 0] = send(view(line, 1, left), ra2.at[line, 0], y_next)
        a1[line, 1].wait_recv()
        add_into(view(line, 3, left, 1), ra1.at[line, 1])
        a2[line, 1] = send(view(line, 3, left), ra2.at[line, 1], y_prev)
    b1[2].wait_recv()
    add_into(view(0, 2, right_cols), rb1.at[2])
    b2 = [
        send(view(0, 2, right_cols, 0), rb2.at[0], y_next),
        send(view(0, 2, right_cols, 1), rb2.at[1], y_prev),
    ]
    b1[1].wait_recv()
    add_into(view(0, 1, right_cols), rb1.at[1])
    b1[3].wait_recv()
    add_into(view(0, 3, right_cols), rb1.at[3])
    a2[1, 0].wait_recv()
    a2[1, 1].wait_recv()
    add_into(view(1, 0, left), ra2.at[1, 0], ra2.at[1, 1])
    a3 = send(view(1, 0, left), ra3, z_other)
    b2[0].wait_recv()
    add_into(view(0, 1, right_cols, 0), rb2.at[0])
    b3 = [send(view(0, 1, right_cols), rb3.at[0], y_next)]
    b2[1].wait_recv()
    add_into(view(0, 3, right_cols, 1), rb2.at[1])
    b3.append(send(view(0, 3, right_cols), rb3.at[1], y_prev))
    a2[0, 0].wait_recv()
    a2[0, 1].wait_recv()
    a3.wait_recv()
    add_into(view(0, 0, left), ra2.at[0, 0], ra2.at[0, 1], ra3)
    own_out.append(move(view(0, 0, left), dx_ref.at[:, left]))
    b1[0].wait_recv()
    b3[0].wait_recv()
    b3[1].wait_recv()
    add_into(view(0, 0, right_cols), rb1.at[0], rb3.at[0], rb3.at[1])
    own_out.append(move(view(0, 0, right_cols), dx_ref.at[:, right_cols]))

    for copy in heads_out:
        copy.wait_recv()
    for copy in own_out:
        copy.wait()
    for copy in sent:
        copy.wait_send()


def per_device(
    queries, key_rows, value_rows, out_grad, moe_input, routes, route_gates, up_weight, down_weight
):
    bins, width = queries.shape[1], queries.shape[2]
    seq_len = bins * 8
    head_cols = width // 8
    hidden = up_weight.shape[2]
    flat = [member.reshape(bins, width) for member in (queries, key_rows, value_rows, out_grad, moe_input)]
    meta = jnp.concatenate([routes[0].astype(F32).T, route_gates[0].T], axis=0)
    any_space = pl.BlockSpec(memory_space=pl.ANY)
    out = jax.ShapeDtypeStruct((bins, width), BF16)
    slot_rows = 2 * CAP
    heads = pltpu.VMEM((seq_len, head_cols), BF16)
    half = width // 2
    results = pl.pallas_call(
        kernel,
        out_shape=(out, out, out, out),
        in_specs=[any_space] * 8,
        out_specs=(any_space,) * 4,
        scratch_shapes=[heads] * 7
        + [
            pltpu.VMEM((seq_len, HD), F32),
            pltpu.VMEM((seq_len, HD), F32),
            pltpu.VMEM((4, 2 * bins, width), BF16),
            pltpu.VMEM((4, 2 * bins, width), BF16),
            pltpu.VMEM((4, 2, 8, bins), F32),
            pltpu.VMEM((4, width, hidden), BF16),
            pltpu.VMEM((4, hidden, width), BF16),
            pltpu.VMEM((4, 4 * slot_rows, width), BF16),
            pltpu.VMEM((4, 4 * slot_rows, width), BF16),
            pltpu.VMEM((4, 4 * slot_rows, 2 * bins), BF16),
            pltpu.VMEM((4, 4 * slot_rows, 128), F32),
            pltpu.VMEM((4 * slot_rows, hidden), BF16),
            pltpu.VMEM((4, 4 * slot_rows, width), BF16),
            pltpu.VMEM((4, 2 * bins, width), BF16),
            pltpu.VMEM((2, 2, bins // 2, half), BF16),
            pltpu.VMEM((2, 2, bins, half), BF16),
            pltpu.VMEM((bins, half), BF16),
            pltpu.VMEM((4, bins, half), BF16),
            pltpu.VMEM((2, bins // 2, half), BF16),
            pltpu.VMEM((2, bins, half), BF16),
            pltpu.SemaphoreType.DMA((N_COPIES,)),
            pltpu.SemaphoreType.DMA((N_COPIES,)),
            pltpu.SemaphoreType.DMA((16,)),
        ],
        compiler_params=pltpu.CompilerParams(
            collective_id=0, has_side_effects=True, vmem_limit_bytes=67043328
        ),
    )(*flat, meta, up_weight, down_weight)
    return tuple(member.reshape(1, bins, width) for member in results)


def solution(mesh):
    rows = P("exp", "ctx", None)
    experts = P("exp", None, None)
    return jax.shard_map(
        per_device,
        mesh=mesh,
        in_specs=(rows,) * 7 + (experts,) * 2,
        out_specs=(rows,) * 4,
        check_vma=False,
    )
```
